32 devices in a mesh: row: 4 (over y, x), col: 8 (over z, core).
Axes of the slice: x: 2, y: 2, z: 4, core: 2. Of those that a mesh axis runs over, the one named last changes fastest.
Arguments:
- left_panel: float32 [4096, 8192], P('col', 'row'), may hold values from -6 to 6
- right_panel: float32 [4096, 16384], P('row', 'col'), may hold values from -0.09375 to 0.09375
- arc_basis: float32 [4096, 256], replicated, as said below
- normal_block: float32 [8192, 16384], P('row', 'col'), may hold values from -6 to 6
Outputs:
- updated_block: float32 [8192, 16384], P('row', 'col')
- left_reduced: float32 [4096, 8192], P('col', 'row')
- right_reduced: float32 [4096, 16384], P('row', 'col')
The draws below stay inside these ranges and needn't reach their ends.
Inputs may be any that keep to these rules, and one draw needn't show every extreme that they name: arc_basis has orthonormal columns: arc_basis^T arc_basis equals the 256 x 256 identity within float32 rounding.
All inputs are finite; a program needn't handle non-finite values.
Results may differ from the reference program's by a relative error of at most 0.00005.
Values sent between devices are 32-bit elements; how exact they have to be, the bound alone decides.
A program may use at most 192 MiB of HBM per device.

```python
import jax
import jax.numpy as jnp
from jax import lax

M = 4096
NL = 8192
NR = 16384
K = 256


def cholesky_pass(columns):
    gram = jnp.dot(columns.T, columns, precision=lax.Precision.HIGHEST, preferred_element_type=jnp.float32)
    factor = jnp.linalg.cholesky(gram)
    solved = jax.scipy.linalg.solve_triangular(factor, columns.T, lower=True)
    return solved.T


def draw_arc_basis(key, part):
    first = jax.random.fold_in(jax.random.fold_in(key, 7301), 0)
    raw = jax.random.normal(first, (M, K), jnp.float32)
    raw = raw * M ** (-0.5)
    return cholesky_pass(cholesky_pass(raw)).astype(jnp.float32)


def levels(key, shape, shards, smallest, largest):
    loudness = 1.0
    for dim, shards_of in shards:
        steps = jax.random.uniform(jax.random.fold_in(jax.random.fold_in(key, 6), dim), (shards_of,), jnp.float32, smallest / len(shards), largest / len(shards))
        loudness = loudness * jnp.repeat(jnp.exp(steps), shape[dim] // shards_of).reshape((-1,) + (1,) * (len(shape) - 1 - dim))
    return loudness


def normal_values(key, shape, scale, reach, cuts=(), dtype=jnp.bfloat16):
    drawn = jax.random.normal(key, shape, jnp.float32) * scale
    if len(cuts) > 0:
        drawn = levels(key, shape, cuts, -0.22, 0.18) * drawn
    return jnp.clip(drawn, min=-reach, max=reach).astype(dtype)


def setup_inputs(seed: int = 0) -> dict:
    keys = jax.random.split(jax.random.key(seed), 5)
    return {
        "left_panel": normal_values(keys[0], (M, NL), 1.0, 6.0, ((0, 8), (1, 4)), jnp.float32),
        "right_panel": normal_values(keys[1], (M, NR), M ** -0.5, 0.09375, ((0, 4), (1, 8)), jnp.float32),
        "arc_basis": draw_arc_basis(jax.random.fold_in(keys[4], 71), 0),
        "normal_block": normal_values(keys[3], (NL, NR), 1.0, 6.0, ((0, 4), (1, 8)), jnp.float32),
    }


def reference(left_panel, right_panel, arc_basis, normal_block):
    highest = lax.Precision.HIGHEST
    left_coef = jnp.dot(arc_basis.T.astype(jnp.float32), left_panel.astype(jnp.float32), precision=highest, preferred_element_type=jnp.float32)
    right_coef = jnp.dot(arc_basis.T.astype(jnp.float32), right_panel.astype(jnp.float32), precision=highest, preferred_element_type=jnp.float32)
    left_reduced = left_panel - jnp.dot(arc_basis.astype(jnp.float32), left_coef.astype(jnp.float32), precision=highest, preferred_element_type=jnp.float32)
    right_reduced = right_panel - jnp.dot(arc_basis.astype(jnp.float32), right_coef.astype(jnp.float32), precision=highest, preferred_element_type=jnp.float32)
    updated_block = normal_block + jnp.dot(left_reduced.T.astype(jnp.float32), right_reduced.astype(jnp.float32), precision=highest, preferred_element_type=jnp.float32)
    return (updated_block, left_reduced, right_reduced)
```

```python
import functools

import jax
import jax.numpy as jnp
from jax import lax
from jax.sharding import PartitionSpec as P


def inner_product(first, second):
    return lax.dot_general(
        first,
        second,
        (((0,), (0,)), ((), ())),
        precision=lax.Precision.HIGH,
        preferred_element_type=jnp.float32,
    )


def plain_product(first, second):
    return jnp.dot(
        first, second, precision=lax.Precision.HIGH, preferred_element_type=jnp.float32
    )


def shift(block, axis, size, distance):
    return lax.ppermute(block, axis, [(i, i ^ distance) for i in range(size)])


def gather_right(owns, rows, row_index):
    if rows != 4:
        return [lax.all_gather(own, "row", axis=0, tiled=True) for own in owns]
    count = owns[0].shape[0]
    half = count // 2
    firsts, seconds, wholes = [], [], []
    for phase, own in enumerate(owns):
        if phase >= 2:
            own, firsts[phase - 2], seconds[phase - 2] = lax.optimization_barrier(
                (own, firsts[phase - 2], seconds[phase - 2])
            )
        firsts.append(shift(own, "row", rows, 1))
        seconds.append(shift(own, "row", rows, 2))
    for own, first, second in zip(owns, firsts, seconds):
        third_top = shift(first[:half], "row", rows, 2)
        third_bottom = shift(second[half:], "row", rows, 1)
        whole = jnp.zeros((rows * count, own.shape[1]), own.dtype)
        for piece, distance, offset in (
            (own, 0, 0),
            (first, 1, 0),
            (second, 2, 0),
            (third_top, 3, 0),
            (third_bottom, 3, half),
        ):
            start = (row_index ^ distance) * count + offset
            whole = lax.dynamic_update_slice_in_dim(whole, piece, start, 0)
        wholes.append(whole)
    return wholes


def local(rows, cols, phases, left_panel, right_panel, arc_basis, normal_block):
    left_count = left_panel.shape[0]
    right_count = right_panel.shape[0]
    per = left_count // phases
    ratio = right_count // left_count
    col_index = lax.axis_index("col")
    row_index = lax.axis_index("row")
    right_split = right_panel.reshape(ratio, left_count, -1)
    basis_split = arc_basis.reshape(cols, left_count, -1)
    spans = [slice(phase * per, (phase + 1) * per) for phase in range(phases)]
    owns = [right_split[:, span].reshape(ratio * per, -1) for span in spans]
    bases = [basis_split[:, span].reshape(cols * per, -1) for span in spans]
    lefts = []
    for span in spans:
        lefts.append(lax.all_gather(left_panel[span], "col", axis=0, tiled=True))
    rights = gather_right(owns, rows, row_index)
    block = normal_block
    left_coef = 0.0
    right_coef = 0.0
    for left, right, basis in zip(lefts, rights, bases):
        right_coef = right_coef + inner_product(basis, right)
        left_coef = left_coef + inner_product(basis, left)
        block = block + inner_product(left, right)
        block, left_coef, right_coef = lax.optimization_barrier(
            (block, left_coef, right_coef)
        )
    basis_left = lax.dynamic_slice_in_dim(arc_basis, col_index * left_count, left_count, 0)
    basis_right = lax.dynamic_slice_in_dim(arc_basis, row_index * right_count, right_count, 0)
    left_reduced = left_panel - plain_product(basis_left, left_coef)
    right_reduced = right_panel - plain_product(basis_right, right_coef)
    updated_block = block - inner_product(left_coef, right_coef)
    return (updated_block, left_reduced, right_reduced)


def solution(mesh):
    rows, cols = mesh.shape["row"], mesh.shape["col"]
    in_specs = (P("col", "row"), P("row", "col"), P(), P("row", "col"))
    out_specs = (P("row", "col"), P("col", "row"), P("row", "col"))
    phases = 4
    return jax.shard_map(
        functools.partial(local, rows, cols, phases),
        mesh=mesh,
        in_specs=in_specs,
        out_specs=out_specs,
        check_vma=False,
    )
```
